256 devices in a mesh: req: 64 (over z, x, core), head: 4 (over y).
Axes of the slice: x: 4, y: 4, z: 8, core: 2. Of those that a mesh axis runs over, the one named last changes fastest.
Arguments:
- hidden: bfloat16 [1536, 1280], P('req'), may hold values from -6 to 6
- w_qkv: bfloat16 [3, 1280, 1280], P(None, None, 'head'), may hold values from -0.15625 to 0.15625
- w_out: bfloat16 [1280, 1280], P('head'), may hold values from -0.15625 to 0.15625
- s_qk: float32 [1280], P('head'), may hold values from 0.5 to 2
- alpha_attn: float32 [1280], replicated, may hold values from 0.05 to 0.5
- w_gate_up: bfloat16 [2, 1280, 2560], P(None, None, 'head'), may hold values from -0.15625 to 0.15625
- w_down: bfloat16 [2560, 1280], P('head'), may hold values from -0.125 to 0.125
- s_up: float32 [2560], P('head'), may hold values from 0.5 to 2
- s_gate: float32 [2560], P('head'), may hold values from 0.5 to 2
- alpha_mlp: float32 [1280], replicated, may hold values from 0.05 to 0.5
- short_keys: bfloat16 [1536, 128, 1280], P('req', None, 'head')
- short_values: bfloat16 [1536, 128, 1280], P('req', None, 'head'), may hold values from -6 to 6
- cache_lengths: int32 [1536], P('req'), may hold values from 1 to 128, as said below
- long_keys: bfloat16 [4, 16384, 1280], P(None, 'req', 'head')
- long_values: bfloat16 [4, 16384, 1280], P(None, 'req', 'head'), may hold values from -6 to 6
- long_rows: int32 [4], replicated, may hold values from 0 to 1535, as said below
Outputs:
- updated: bfloat16 [1536, 1280], P('req')
The draws below stay inside these ranges and needn't reach their ends.
Inputs may be any that keep to these rules, and one draw needn't show every extreme that they name: `cache_lengths`: the entries of the rows named by long_rows are not read. `long_rows`: 4 distinct request rows.
All inputs are finite; a program needn't handle non-finite values.
Results may differ from the reference program's by a relative error of at most 0.011.
Values may be sent and summed in bfloat16 or wider, within the bound.
A program may use at most 64 MiB of HBM per device.

```python
import math
import jax
import jax.numpy as jnp
from jax import lax

D = 1280
HEADS = 20
HEAD_DIM = 64
FF = 2560
SHORT = 128
LONGS = 4
REQ_DEV = 24
LONG_DEV = 256
REQS = 1536
LONG = 16384


def pick_long_rows(key):
    inner = jax.random.permutation(jax.random.fold_in(key, 11), REQS - 2)[:LONGS - 2].astype(jnp.int32) + 1
    ends = jnp.array([0, REQS - 1], dtype=jnp.int32)
    chosen = jnp.concatenate([ends, inner])
    order = jax.random.permutation(jax.random.fold_in(key, 13), LONGS)
    return chosen[order].astype(jnp.int32)


def draw_short_keys(key, part):
    shape = (REQS, SHORT, D)
    base = jax.random.normal(jax.random.fold_in(key, 1), shape, jnp.float32) * 0.125
    return base.astype(jnp.bfloat16)


def draw_long_keys(key, part):
    blocks = LONG // LONG_DEV
    chosen = pick_long_rows(key)
    owner = chosen // REQ_DEV
    offset = jax.random.randint(jax.random.fold_in(key, 3), (LONGS,), 1, blocks, dtype=jnp.int32)
    strongest = (owner + offset) % blocks
    low_level = 0.0
    base = jax.random.normal(jax.random.fold_in(key, 1), (LONGS, blocks, LONG_DEV, D), jnp.float32) * 0.125
    levels = jnp.exp(jax.random.uniform(jax.random.fold_in(key, 5), (LONGS, blocks), jnp.float32, low_level, math.log(100.0)))
    block_ids = jnp.arange(blocks, dtype=jnp.int32)[None, :]
    levels = jnp.where(block_ids == strongest[:, None], 100.0, levels)
    quiet = jnp.exp(jax.random.uniform(jax.random.fold_in(key, 9), (LONGS, blocks), jnp.float32, math.log(0.5), 0.0))
    levels = jnp.where(block_ids == owner[:, None], quiet, levels)
    keys = base * levels[:, :, None, None]
    return keys.reshape(LONGS, LONG, D).astype(jnp.bfloat16)


def draw_cache_lengths(key, part):
    values = jax.random.randint(key, (REQS,), 1, SHORT + 1, dtype=jnp.int32)
    where = jax.random.randint(jax.random.fold_in(key, 3), (), 0, REQS, dtype=jnp.int32)
    return values.at[where].set(SHORT)


def draw_long_rows(key, part):
    return pick_long_rows(key)


def block_scale(own_key, shape, pieces, least, largest):
    def one(axis_at, parts):
        heights = jax.random.uniform(jax.random.fold_in(jax.random.fold_in(own_key, 6), axis_at), (parts,), jnp.float32, least / len(pieces), largest / len(pieces))
        return jnp.repeat(jnp.exp(heights), shape[axis_at] // parts).reshape((-1,) + (1,) * (len(shape) - axis_at - 1))

    factor_of = one(*pieces[0])
    for cut in pieces[1:]:
        factor_of = factor_of * one(*cut)
    return factor_of


def noise(stream_key, dims, scale, reach, pieces=(), kind=jnp.bfloat16):
    values = scale * jax.random.normal(stream_key, dims, jnp.float32)
    if pieces:
        values = values * block_scale(stream_key, dims, pieces, -0.22, 0.18)
    return jnp.clip(values, -reach, reach).astype(kind)


def setup_inputs(seed: int = 0) -> dict:
    key_of = jax.random.split(jax.random.key(seed), 17)
    return {
        "hidden": noise(key_of[0], (REQS, D), 1.0, 6.0, ((0, 64),)),
        "w_qkv": noise(key_of[1], (3, D, D), D ** -0.5, 0.15625, ((2, 4),)),
        "w_out": noise(key_of[2], (D, D), D ** -0.5, 0.15625, ((0, 4),)),
        "s_qk": jnp.clip(jnp.exp(math.log(2.0) - 1.3862944 * jax.random.uniform(key_of[3], (D,), jnp.float32) ** block_scale(key_of[3], (D,), ((0, 4),), -0.2, 0.2)), 0.5, 2.0),
        "alpha_attn": jnp.clip(jnp.exp(jax.random.uniform(key_of[4], (D,), jnp.float32, math.log(0.05), math.log(0.5))), 0.05, 0.5),
        "w_gate_up": noise(key_of[5], (2, D, FF), D ** -0.5, 0.15625, ((2, 4),)),
        "w_down": noise(key_of[6], (FF, D), FF ** -0.5, 0.125, ((0, 4),)),
        "s_up": jnp.clip(jnp.exp(math.log(2.0) - 1.3862944 * jax.random.uniform(key_of[7], (FF,), jnp.float32) ** block_scale(key_of[7], (FF,), ((0, 4),), -0.2, 0.2)), 0.5, 2.0),
        "s_gate": jnp.clip(jnp.exp(math.log(2.0) - 1.3862944 * jax.random.uniform(key_of[8], (FF,), jnp.float32) ** block_scale(key_of[8], (FF,), ((0, 4),), -0.2, 0.2)), 0.5, 2.0),
        "alpha_mlp": jnp.clip(jnp.exp(jax.random.uniform(key_of[9], (D,), jnp.float32, math.log(0.05), math.log(0.5))), 0.05, 0.5),
        "short_keys": draw_short_keys(jax.random.fold_in(key_of[16], 71), 0),
        "short_values": noise(key_of[11], (REQS, SHORT, D), 1.0, 6.0, ((0, 64), (2, 4))),
        "cache_lengths": draw_cache_lengths(jax.random.fold_in(key_of[16], 71), 0),
        "long_keys": draw_long_keys(jax.random.fold_in(key_of[16], 71), 0),
        "long_values": noise(key_of[14], (LONGS, LONG, D), 1.0, 6.0, ((1, 64), (2, 4))),
        "long_rows": draw_long_rows(jax.random.fold_in(key_of[16], 71), 0),
    }


EPS = 1e-06

def row_norm(values):
    return values * lax.rsqrt(lax.optimization_barrier(jnp.mean(values * values, axis=-1, keepdims=True)) + EPS)

def head_unit(values, gains):
    shaped = values.reshape(values.shape[:-1] + (HEADS, HEAD_DIM))
    scaled = shaped * lax.rsqrt(lax.optimization_barrier(jnp.sum(shaped * shaped, axis=-1, keepdims=True)) + EPS)
    return scaled.reshape(values.shape) * gains

def attend_one(query, key_new, value_new, keys, values, valid):
    query32 = query.astype(jnp.float32)
    scale = math.sqrt(HEAD_DIM)
    scores = scale * jnp.einsum('hd,jhd->hj', query32, keys.astype(jnp.float32))
    scores = jnp.where(valid[None, :], scores, -1e+30)
    own = scale * lax.optimization_barrier(jnp.sum(query32 * key_new.astype(jnp.float32), axis=-1))
    top = jnp.maximum(lax.optimization_barrier(jnp.max(scores, axis=-1)), own)
    weights = jnp.where(valid[None, :], jnp.exp(scores - top[:, None]), 0.0)
    own_weight = jnp.exp(own - top)
    total = lax.optimization_barrier(jnp.sum(weights, axis=-1)) + own_weight
    summed = jnp.einsum('hj,jhd->hd', weights.astype(jnp.bfloat16).astype(jnp.float32), values.astype(jnp.float32))
    summed = summed + own_weight.astype(jnp.bfloat16).astype(jnp.float32)[:, None] * value_new.astype(jnp.float32)
    return summed / total[:, None]

def reference(hidden, w_qkv, w_out, s_qk, alpha_attn, w_gate_up, w_down, s_up, s_gate, alpha_mlp, short_keys, short_values, cache_lengths, long_keys, long_values, long_rows):
    query = jnp.dot(hidden, w_qkv[0], preferred_element_type=jnp.float32)
    key_new = jnp.dot(hidden, w_qkv[1], preferred_element_type=jnp.float32)
    value_new = jnp.dot(hidden, w_qkv[2], preferred_element_type=jnp.float32)
    query_unit = head_unit(query, s_qk).astype(jnp.bfloat16).reshape(REQS, HEADS, HEAD_DIM)
    key_unit = head_unit(key_new, s_qk).astype(jnp.bfloat16).reshape(REQS, HEADS, HEAD_DIM)
    value_heads = value_new.astype(jnp.bfloat16).reshape(REQS, HEADS, HEAD_DIM)
    blocks = REQS // 8
    valid = jnp.arange(SHORT, dtype=jnp.int32)[None, :] < cache_lengths[:, None]

    def block_fn(packed):
        return jax.vmap(attend_one)(*packed)
    packed = (query_unit.reshape(blocks, 8, HEADS, HEAD_DIM), key_unit.reshape(blocks, 8, HEADS, HEAD_DIM), value_heads.reshape(blocks, 8, HEADS, HEAD_DIM), short_keys.reshape(blocks, 8, SHORT, HEADS, HEAD_DIM), short_values.reshape(blocks, 8, SHORT, HEADS, HEAD_DIM), valid.reshape(blocks, 8, SHORT))
    attended = lax.map(block_fn, packed).reshape(REQS, HEADS, HEAD_DIM)
    always = jnp.ones((LONG,), dtype=bool)
    for index in range(LONGS):
        row = long_rows[index]
        result = attend_one(query_unit[row], key_unit[row], value_heads[row], long_keys[index].reshape(LONG, HEADS, HEAD_DIM), long_values[index].reshape(LONG, HEADS, HEAD_DIM), always)
        attended = attended.at[row].set(result)
    attended = attended.astype(jnp.bfloat16).reshape(REQS, D)
    base = hidden.astype(jnp.float32)
    projected = jnp.dot(attended, w_out, preferred_element_type=jnp.float32)
    middle = row_norm(base + alpha_attn * (row_norm(projected) - base)).astype(jnp.bfloat16)
    gate = jnp.dot(middle, w_gate_up[0], preferred_element_type=jnp.float32) * s_gate
    upward = jnp.dot(middle, w_gate_up[1], preferred_element_type=jnp.float32) * s_up
    gated = (jax.nn.silu(gate) * upward).astype(jnp.bfloat16)
    downward = jnp.dot(gated, w_down, preferred_element_type=jnp.float32)
    middle32 = middle.astype(jnp.float32)
    return row_norm(middle32 + alpha_mlp * (row_norm(downward) - middle32)).astype(jnp.bfloat16)
```

```python
import functools
import math

import jax
import jax.numpy as jnp
from jax import lax
from jax.experimental import pallas as pl
from jax.experimental.pallas import tpu as pltpu
from jax.sharding import PartitionSpec as P

HEAD_DIM = 64
EPS = 1e-06
NEAR = 8
LANES = 128
GROUP = 8
MESH = pl.DeviceIdType.MESH
F32 = jnp.float32
BF16 = jnp.bfloat16
LOW = -1e30


def iota(shape, axis):
    return lax.broadcasted_iota(jnp.int32, shape, axis)


def dot(a, b):
    return jnp.dot(a, b, preferred_element_type=F32)


def dot_t(a, b):
    return lax.dot_general(a, b, (((1,), (1,)), ((), ())), preferred_element_type=F32)


def row_norm(values):
    return values * lax.rsqrt(jnp.mean(values * values, axis=-1, keepdims=True) + EPS)


def head_unit(values, gains, same_head):
    squares = values * values
    high = squares.astype(BF16)
    low = (squares - high.astype(F32)).astype(BF16)
    sums = dot(high, same_head) + dot(low, same_head)
    return values * lax.rsqrt(sums + EPS) * gains


def split3(values):
    high = values.astype(BF16).astype(F32)
    rest = values - high
    middle = rest.astype(BF16).astype(F32)
    return high, middle, (rest - middle).astype(BF16).astype(F32)


def pack_heads(wide):
    upper = iota((GROUP, LANES), 0) < 4
    first = jnp.where(upper, wide[:, :LANES], pltpu.roll(wide[:, LANES : 2 * LANES], 4, 0))
    return jnp.concatenate([first, wide[:, 2 * LANES :]], axis=0).astype(BF16)


def kernel(near, far, heads, *refs):
    (
        rows_hbm, lens_hbm, hid_hbm, wqkv_hbm, sqk_hbm, sk_hbm, sv_hbm, lk_hbm, lv_hbm, wout_hbm, aat_hbm,
        wgu_hbm, sgate_hbm, sup_hbm, wdn_hbm, aml_hbm, out_ref,
        rows_s, lens_s, hid_v, wqkv_v, sqk_v, sk_v, sv_v, lk_v, lv_v, wout_v, aat_v,
        wgu_v, sgate_v, sup_v, wdn_v, aml_v,
        qbd_v, vb_v, s_v, o_v, lqbd_v, ls_v, lo_v, wide_v, att_v, mid_v, new_v,
        xq1, xq2, xp1, xp2, ys1, ys2, yl1, yl2,
        load_sem, send_sem, recv_sem,
    ) = refs
    me_req = lax.axis_index("req")
    me_head = lax.axis_index("head")
    me_near = lax.rem(me_req, near)
    me_far = lax.div(me_req, near)
    rows = hid_v.shape[0]
    width = sqk_v.shape[0]
    longs = lk_v.shape[0]
    scale = math.sqrt(HEAD_DIM)

    def near_peer(d):
        return {"req": me_far * near + lax.rem(me_near + d, near), "head": me_head}

    def far_peer(d):
        return {"req": lax.rem(me_far + d, far) * near + me_near, "head": me_head}

    def head_peer(d):
        return {"req": me_req, "head": lax.rem(me_head + d, heads)}

    barrier = pltpu.get_barrier_semaphore()
    for count, peer in ((far, far_peer), (near, near_peer), (heads, head_peer)):
        for d in range(1, count):
            pl.semaphore_signal(barrier, inc=1, device_id=peer(d), device_id_type=MESH)

    loads = {}

    def load(name, src, dst):
        copy = pltpu.make_async_copy(src, dst, load_sem.at[len(loads)])
        copy.start()
        loads[name] = copy

    load("rows", rows_hbm, rows_s)
    load("hid", hid_hbm, hid_v)
    load("wq", wqkv_hbm.at[0], wqkv_v.at[0])
    load("sqk", sqk_hbm, sqk_v)
    load("lens", lens_hbm, lens_s)
    load("wk", wqkv_hbm.at[1], wqkv_v.at[1])
    load("wv", wqkv_hbm.at[2], wqkv_v.at[2])
    load("sk", sk_hbm, sk_v)
    load("sv", sv_hbm, sv_v)
    load("lk", lk_hbm, lk_v)
    load("lv", lv_hbm, lv_v)
    load("wout", wout_hbm, wout_v)
    load("aat", aat_hbm, aat_v)
    load("wgu", wgu_hbm, wgu_v)
    load("sgate", sgate_hbm, sgate_v)
    load("sup", sup_hbm, sup_v)
    load("wdn", wdn_hbm, wdn_v)
    load("aml", aml_hbm, aml_v)

    sent = []

    def exchange(slot, slots, count, me, peer):
        order = sorted(range(1, count), key=lambda d: -min(d, count - d))
        copies = []
        for d in order:
            copy = pltpu.make_async_remote_copy(
                src_ref=slots.at[me],
                dst_ref=slots.at[me],
                send_sem=send_sem.at[slot, d],
                recv_sem=recv_sem.at[slot, d],
                device_id=peer(d),
                device_id_type=MESH,
            )
            copy.start()
            copies.append(copy)
        sent.extend(copies)

        def arrive():
            for copy in copies:
                copy.wait_recv()

        return arrive

    same_head = (iota((width, width), 0) // HEAD_DIM == iota((width, width), 1) // HEAD_DIM).astype(BF16)
    total = rows * GROUP
    spread = (iota((total, rows), 0) // GROUP == iota((total, rows), 1)).astype(BF16)
    gather = (iota((rows, total), 1) // GROUP == iota((rows, total), 0)).astype(BF16)
    own_lanes = iota((total, width), 0) % GROUP == iota((total, width), 1) // HEAD_DIM
    ltotal = longs * GROUP
    lspread = (iota((ltotal, GROUP), 0) // GROUP == iota((ltotal, GROUP), 1)).astype(BF16)
    lgather = (iota((GROUP, ltotal), 1) // GROUP == iota((GROUP, ltotal), 0)).astype(BF16)
    lown_lanes = iota((ltotal, width), 0) % GROUP == iota((ltotal, width), 1) // HEAD_DIM
    sub = iota((GROUP, LANES), 0)
    lane = iota((GROUP, LANES), 1)

    for name in ("rows", "hid", "wq", "sqk"):
        loads[name].wait()
    offset = me_req * rows
    local = [rows_s[i] - offset for i in range(longs)]
    gains = sqk_v[...].reshape(1, width)
    hidden = hid_v[...]
    query = head_unit(dot_t(hidden, wqkv_v[0]), gains, same_head).astype(BF16)
    column = jnp.full((GROUP, rows), -1, jnp.int32)
    for i in range(longs):
        column = jnp.where(iota((GROUP, rows), 0) == i, local[i], column)
    pick = (column == iota((GROUP, rows), 1)).astype(BF16)
    wide_v[:, 2 * LANES :] = jnp.zeros((GROUP, LANES), F32)
    wide_v[:, :width] = dot(pick, query)
    xq1[me_near] = pack_heads(wide_v[...])
    pl.semaphore_wait(barrier, near + far + heads - 3)
    arrive = exchange(0, xq1, near, me_near, near_peer)

    loads["wk"].wait()
    key = head_unit(dot_t(hidden, wqkv_v[1]), gains, same_head).astype(BF16)
    loads["wv"].wait()
    value = dot_t(hidden, wqkv_v[2]).astype(BF16)
    picked_key = dot(pick, key).astype(BF16)
    picked_value = dot(pick, value).astype(BF16)
    picked_hidden = dot(pick, hidden)
    query_rows = jnp.where(own_lanes, dot(spread, query), 0.0)
    qbd_v[...] = query_rows
    own = scale * jnp.sum(query_rows * dot(spread, key), axis=-1, keepdims=True)
    vb_v[...] = dot(spread, value)
    loads["lens"].wait()
    loads["sk"].wait()
    slots = sk_v.shape[2]
    for r in range(rows):
        block = slice(r * GROUP, (r + 1) * GROUP)
        part = scale * dot(qbd_v[block, :].astype(BF16), sk_v[r])
        s_v[block, :] = jnp.where(iota((GROUP, slots), 1) < lens_s[r], part, LOW)

    arrive()

    def sum_slots(ref, count):
        acc = ref[0].astype(F32)
        for i in range(1, count):
            acc = acc + ref[i].astype(F32)
        return acc

    xq2[me_far] = sum_slots(xq1, near).astype(BF16)
    arrive = exchange(1, xq2, far, me_far, far_peer)

    scores = s_v[...]
    top = jnp.maximum(jnp.max(scores, axis=-1, keepdims=True), own)
    weights = jnp.exp(scores - top)
    own_weight = jnp.exp(own - top)
    share = 1.0 / (jnp.sum(weights, axis=-1, keepdims=True) + own_weight)
    s_v[...] = weights
    loads["sv"].wait()
    for r in range(rows):
        block = slice(r * GROUP, (r + 1) * GROUP)
        o_v[block, :] = dot_t(s_v[block, :].astype(BF16), sv_v[r])
    summed = o_v[...] + own_weight.astype(BF16).astype(F32) * vb_v[...]
    blocks = jnp.where(own_lanes, summed * share, 0.0).astype(BF16)
    attended = dot(gather, blocks).astype(BF16)
    loads["wout"].wait()
    ys1[me_head] = dot(attended, wout_v[...]).astype(BF16)
    short_arrive = exchange(2, ys1, heads, me_head, head_peer)

    loads["lk"].wait()
    loads["lv"].wait()
    arrive()
    queries = sum_slots(xq2, far)

    def unpack_heads(first, second):
        wide_v[:, :LANES] = first
        wide_v[:, LANES : 2 * LANES] = pltpu.roll(first, 4, 0)
        wide_v[:, 2 * LANES :] = second
        return jnp.where(iota((GROUP, width), 0) < 4, wide_v[:, :width], 0.0).astype(BF16)

    long_query = unpack_heads(queries[:GROUP], queries[GROUP:])
    long_rows = jnp.where(lown_lanes, dot(lspread, long_query), 0.0)
    lqbd_v[...] = long_rows
    for i in range(longs):
        block = slice(i * GROUP, (i + 1) * GROUP)
        ls_v[block, :] = scale * dot(lqbd_v[block, :].astype(BF16), lk_v[i])
    place = jnp.full((ltotal, 1), -1, jnp.int32)
    for i in range(longs):
        place = jnp.where(iota((ltotal, 1), 0) // GROUP == i, local[i], place)
    owner = (place >= 0) & (place < rows)
    long_own = scale * jnp.sum(long_rows * dot(lspread, picked_key), axis=-1, keepdims=True)
    long_own = jnp.where(owner, long_own, LOW)
    long_scores = ls_v[...]
    long_top = jnp.maximum(jnp.max(long_scores, axis=-1, keepdims=True), long_own)
    long_weights = jnp.exp(long_scores - long_top)
    long_own_weight = jnp.where(owner, jnp.exp(long_own - long_top), 0.0)
    long_total = jnp.sum(long_weights, axis=-1, keepdims=True) + long_own_weight
    ls_v[...] = long_weights
    for i in range(longs):
        block = slice(i * GROUP, (i + 1) * GROUP)
        lo_v[block, :] = dot_t(ls_v[block, :].astype(BF16), lv_v[i])
    long_summed = lo_v[...] + long_own_weight.astype(BF16).astype(F32) * dot(lspread, picked_value)
    long_blocks = jnp.where(lown_lanes, long_summed / long_total, 0.0).astype(BF16)
    tops = split3(long_top + jnp.log(long_total))
    wide_lane = iota((ltotal, LANES), 1) - HEAD_DIM - iota((ltotal, LANES), 0) % GROUP
    placed = jnp.zeros((ltotal, LANES), F32)
    for i in range(3):
        placed = jnp.where(wide_lane == i * GROUP, tops[i], placed)
    wide_v[:, 2 * LANES :] = dot(lgather, placed.astype(BF16))
    wide_v[:, :width] = dot(lgather, long_blocks)
    xp1[me_near] = pack_heads(wide_v[...])
    arrive = exchange(3, xp1, near, me_near, near_peer)

    for name in ("aat", "wgu", "sgate", "sup", "wdn", "aml"):
        loads[name].wait()
    alpha_attn = aat_v[...].reshape(1, -1)
    alpha_mlp = aml_v[...].reshape(1, -1)
    gate_gain = sgate_v[...].reshape(1, -1)
    up_gain = sup_v[...].reshape(1, -1)

    def update(summed, base, alpha):
        return row_norm(base + alpha * (row_norm(summed) - base)).astype(BF16)

    def feed_forward(middle):
        gate = dot(middle, wgu_v[0]) * gate_gain
        upward = dot(middle, wgu_v[1]) * up_gain
        gated = (gate / (1.0 + jnp.exp(-gate)) * upward).astype(BF16)
        return dot(gated, wdn_v[...])

    short_arrive()
    mid_v[...] = update(sum_slots(ys1, heads), hidden.astype(F32), alpha_attn)

    def merge(ref, count):
        firsts, seconds, sums = [], [], []
        for i in range(count):
            both = ref[i].astype(F32)
            second = both[GROUP:]
            firsts.append(both[:GROUP])
            seconds.append(second)
            sums.append(
                second + pltpu.roll(second, LANES - GROUP, 1) + pltpu.roll(second, LANES - 2 * GROUP, 1)
            )
        most = functools.reduce(jnp.maximum, sums)
        parts = [jnp.exp(s - most) for s in sums]
        whole = functools.reduce(jnp.add, parts)
        out_first = jnp.zeros((GROUP, LANES), F32)
        out_second = jnp.zeros((GROUP, LANES), F32)
        for i in range(count):
            ratio = parts[i] / whole
            turned = pltpu.roll(pltpu.roll(ratio, 4, 0), LANES - 2, 1)
            mixed = jnp.where(sub < 4, ratio, turned)
            left = mixed[:, HEAD_DIM : HEAD_DIM + 1]
            right = mixed[:, HEAD_DIM + 1 : HEAD_DIM + 2]
            out_first = out_first + jnp.where(lane < HEAD_DIM, left, right) * firsts[i]
            out_second = out_second + ratio[:, HEAD_DIM + 4 : HEAD_DIM + 5] * seconds[i]
        return out_first, out_second, most + jnp.log(whole)

    arrive()
    first, second, logs = merge(xp1, near)
    high, middle, low = split3(logs)
    second = jnp.where(lane < HEAD_DIM, second, 0.0)
    lanes_of = ((0, high), (1, pltpu.roll(middle, GROUP, 1)), (2, pltpu.roll(low, 2 * GROUP, 1)))
    for i, term in lanes_of:
        inside = (lane >= HEAD_DIM + i * GROUP) & (lane < HEAD_DIM + (i + 1) * GROUP)
        second = jnp.where(inside, term, second)
    xp2[me_far] = jnp.concatenate([first, second], axis=0).astype(BF16)
    arrive = exchange(4, xp2, far, me_far, far_peer)

    ys2[me_head] = feed_forward(mid_v[...]).astype(BF16)
    short_arrive = exchange(5, ys2, heads, me_head, head_peer)

    half = hidden.shape[1] // 2

    def pack_rows(values):
        upper = iota((GROUP, half), 0) < 4
        return jnp.where(upper, values[:, :half], pltpu.roll(values[:, half:], 4, 0)).astype(BF16)

    def unpack_rows(packed):
        return jnp.concatenate([packed, pltpu.roll(packed, 4, 0)], axis=1)

    arrive()
    first, second, _ = merge(xp2, far)
    long_attended = unpack_heads(first, second)
    yl1[me_head] = pack_rows(dot(long_attended, wout_v[...]))
    arrive = exchange(6, yl1, heads, me_head, head_peer)

    short_arrive()
    new_v[...] = update(sum_slots(ys2, heads), mid_v[...].astype(F32), alpha_mlp)

    arrive()
    long_middle = update(unpack_rows(sum_slots(yl1, heads)), picked_hidden, alpha_attn)
    yl2[me_head] = pack_rows(feed_forward(long_middle))
    arrive = exchange(7, yl2, heads, me_head, head_peer)
    arrive()
    long_new = update(unpack_rows(sum_slots(yl2, heads)), long_middle.astype(F32), alpha_mlp).astype(F32)
    result = new_v[...].astype(F32)
    for i in range(longs):
        here = iota((rows, result.shape[1]), 0) == local[i]
        result = jnp.where(here, long_new[i : i + 1, :], result)
    out_ref[...] = result.astype(BF16)
    for copy in sent:
        copy.wait_send()


def on_device(
    near,
    far,
    heads,
    hidden,
    w_qkv,
    w_out,
    s_qk,
    alpha_attn,
    w_gate_up,
    w_down,
    s_up,
    s_gate,
    alpha_mlp,
    short_keys,
    short_values,
    cache_lengths,
    long_keys,
    long_values,
    long_rows,
):
    def turned(array):
        return jnp.transpose(array, (0, 2, 1))

    arguments = (
        long_rows, cache_lengths, hidden, turned(w_qkv), s_qk, turned(short_keys), turned(short_values),
        turned(long_keys), turned(long_values), w_out, alpha_attn, w_gate_up, s_gate, s_up, w_down, alpha_mlp,
    )
    rows, model = hidden.shape
    width = w_qkv.shape[2]
    slots, longs, span = short_keys.shape[1], long_keys.shape[0], long_keys.shape[1]
    copies = [
        (pltpu.SMEM if a.dtype == jnp.int32 else pltpu.VMEM)(a.shape, a.dtype) for a in arguments
    ]
    return pl.pallas_call(
        functools.partial(kernel, near, far, heads),
        out_shape=jax.ShapeDtypeStruct(hidden.shape, BF16),
        in_specs=[pl.BlockSpec(memory_space=pl.ANY)] * len(arguments),
        out_specs=pl.BlockSpec(memory_space=pltpu.VMEM),
        scratch_shapes=copies
        + [
            pltpu.VMEM((rows * GROUP, width), F32),
            pltpu.VMEM((rows * GROUP, width), F32),
            pltpu.VMEM((rows * GROUP, slots), F32),
            pltpu.VMEM((rows * GROUP, width), F32),
            pltpu.VMEM((longs * GROUP, width), F32),
            pltpu.VMEM((longs * GROUP, span), F32),
            pltpu.VMEM((longs * GROUP, width), F32),
            pltpu.VMEM((GROUP, 3 * LANES), F32),
            pltpu.VMEM((rows, width), BF16),
            pltpu.VMEM((rows, model), BF16),
            pltpu.VMEM((rows, model), BF16),
            pltpu.VMEM((near, 2 * GROUP, LANES), BF16),
            pltpu.VMEM((far, 2 * GROUP, LANES), BF16),
            pltpu.VMEM((near, 2 * GROUP, LANES), BF16),
            pltpu.VMEM((far, 2 * GROUP, LANES), BF16),
            pltpu.VMEM((heads, rows, model), BF16),
            pltpu.VMEM((heads, rows, model), BF16),
            pltpu.VMEM((heads, GROUP, model // 2), BF16),
            pltpu.VMEM((heads, GROUP, model // 2), BF16),
            pltpu.SemaphoreType.DMA((len(arguments) + 2,)),
            pltpu.SemaphoreType.DMA((8, 8)),
            pltpu.SemaphoreType.DMA((8, 8)),
        ],
        compiler_params=pltpu.CompilerParams(collective_id=0, has_side_effects=True),
    )(*arguments)


def solution(mesh):
    reqs, heads = mesh.shape["req"], mesh.shape["head"]
    near = math.gcd(NEAR, reqs)
    return jax.shard_map(
        functools.partial(on_device, near, reqs // near, heads),
        mesh=mesh,
        in_specs=(
            P("req", None),
            P(None, None, "head"),
            P("head", None),
            P("head"),
            P(),
            P(None, None, "head"),
            P("head", None),
            P("head"),
            P("head"),
            P(),
            P("req", None, "head"),
            P("req", None, "head"),
            P("req"),
            P(None, "req", "head"),
            P(None, "req", "head"),
            P(),
        ),
        out_specs=P("req", None),
        check_vma=False,
    )
```

```python
import functools
import math

import jax
import jax.numpy as jnp
from jax import lax
from jax.experimental import pallas as pl
from jax.experimental.pallas import tpu as pltpu
from jax.sharding import PartitionSpec as P

HEAD_DIM = 64
EPS = 1e-06
NEAR = 8
LANES = 128
GROUP = 8
MESH = pl.DeviceIdType.MESH
F32 = jnp.float32
BF16 = jnp.bfloat16
LOW = -1e30


def iota(shape, axis):
    return lax.broadcasted_iota(jnp.int32, shape, axis)


def dot(a, b):
    return jnp.dot(a, b, preferred_element_type=F32)


def dot_t(a, b):
    return lax.dot_general(a, b, (((1,), (1,)), ((), ())), preferred_element_type=F32)


def row_norm(values):
    return values * lax.rsqrt(jnp.mean(values * values, axis=-1, keepdims=True) + EPS)


def head_unit(values, gains, same_head):
    squares = values * values
    high = squares.astype(BF16)
    low = (squares - high.astype(F32)).astype(BF16)
    sums = dot(high, same_head) + dot(low, same_head)
    return values * lax.rsqrt(sums + EPS) * gains


def split3(values):
    high = values.astype(BF16).astype(F32)
    rest = values - high
    middle = rest.astype(BF16).astype(F32)
    return high, middle, (rest - middle).astype(BF16).astype(F32)


def pack_heads(wide):
    upper = iota((GROUP, LANES), 0) < 4
    first = jnp.where(upper, wide[:, :LANES], pltpu.roll(wide[:, LANES : 2 * LANES], 4, 0))
    return jnp.concatenate([first, wide[:, 2 * LANES :]], axis=0).astype(BF16)


def kernel(near, far, heads, *refs):
    (
        rows_hbm, lens_hbm, hid_hbm, wqkv_hbm, sqk_hbm, sk_hbm, sv_hbm, lk_hbm, lv_hbm, wout_hbm, aat_hbm,
        wgu_hbm, sgate_hbm, sup_hbm, wdn_hbm, aml_hbm, out_ref,
        rows_s, lens_s, hid_v, wqkv_v, sqk_v, sk_v, sv_v, lk_v, lv_v, wout_v, aat_v,
        wgu_v, sgate_v, sup_v, wdn_v, aml_v,
        qbd_v, vb_v, s_v, o_v, lqbd_v, ls_v, lo_v, wide_v, att_v, mid_v, new_v,
        xq1, xq2, xp1, xp2, ys1, ys2, yl1, yl2,
        load_sem, send_sem, recv_sem,
    ) = refs
    me_req = lax.axis_index("req")
    me_head = lax.axis_index("head")
    me_near = lax.rem(me_req, near)
    me_far = lax.div(me_req, near)
    rows = hid_v.shape[0]
    width = sqk_v.shape[0]
    longs = lk_v.shape[0]
    scale = math.sqrt(HEAD_DIM)

    def near_peer(d):
        return {"req": me_far * near + lax.rem(me_near + d, near), "head": me_head}

    def far_peer(d):
        return {"req": lax.rem(me_far + d, far) * near + me_near, "head": me_head}

    def head_peer(d):
        return {"req": me_req, "head": lax.rem(me_head + d, heads)}

    barrier = pltpu.get_barrier_semaphore()
    for count, peer in ((far, far_peer), (near, near_peer), (heads, head_peer)):
        for d in range(1, count):
            pl.semaphore_signal(barrier, inc=1, device_id=peer(d), device_id_type=MESH)

    loads = {}

    def load(name, src, dst):
        copy = pltpu.make_async_copy(src, dst, load_sem.at[len(loads)])
        copy.start()
        loads[name] = copy

    load("hid", hid_hbm, hid_v)
    load("rows", rows_hbm, rows_s)
    load("wq", wqkv_hbm.at[0], wqkv_v.at[0])
    load("sqk", sqk_hbm, sqk_v)

    load("lens", lens_hbm, lens_s)
    load("wk", wqkv_hbm.at[1], wqkv_v.at[1])
    load("wv", wqkv_hbm.at[2], wqkv_v.at[2])
    load("sk", sk_hbm, sk_v)
    load("sv", sv_hbm, sv_v)
    load("lk", lk_hbm, lk_v)
    load("lv", lv_hbm, lv_v)
    load("wout", wout_hbm, wout_v)
    load("aat", aat_hbm, aat_v)
    load("wgu", wgu_hbm, wgu_v)
    load("sgate", sgate_hbm, sgate_v)
    load("sup", sup_hbm, sup_v)
    load("wdn", wdn_hbm, wdn_v)
    load("aml", aml_hbm, aml_v)

    sent = []

    def exchange(slot, slots, count, me, peer):
        order = sorted(range(1, count), key=lambda d: -min(d, count - d))
        copies = []
        for d in order:
            copy = pltpu.make_async_remote_copy(
                src_ref=slots.at[me],
                dst_ref=slots.at[me],
                send_sem=send_sem.at[slot, d],
                recv_sem=recv_sem.at[slot, d],
                device_id=peer(d),
                device_id_type=MESH,
            )
            copy.start()
            copies.append(copy)
        sent.extend(copies)

        def arrive():
            for copy in copies:
                copy.wait_recv()

        return arrive

    same_head = (iota((width, width), 0) // HEAD_DIM == iota((width, width), 1) // HEAD_DIM).astype(BF16)
    total = rows * GROUP
    spread = (iota((total, rows), 0) // GROUP == iota((total, rows), 1)).astype(BF16)
    gather = (iota((rows, total), 1) // GROUP == iota((rows, total), 0)).astype(BF16)
    own_lanes = iota((total, width), 0) % GROUP == iota((total, width), 1) // HEAD_DIM
    ltotal = longs * GROUP
    lspread = (iota((ltotal, GROUP), 0) // GROUP == iota((ltotal, GROUP), 1)).astype(BF16)
    lgather = (iota((GROUP, ltotal), 1) // GROUP == iota((GROUP, ltotal), 0)).astype(BF16)
    lown_lanes = iota((ltotal, width), 0) % GROUP == iota((ltotal, width), 1) // HEAD_DIM
    sub = iota((GROUP, LANES), 0)
    lane = iota((GROUP, LANES), 1)

    for name in ("rows", "hid"):
        loads[name].wait()
    offset = me_req * rows
    local = [rows_s[i] - offset for i in range(longs)]
    hidden = hid_v[...]
    column = jnp.full((GROUP, rows), -1, jnp.int32)
    for i in range(longs):
        column = jnp.where(iota((GROUP, rows), 0) == i, local[i], column)
    pick = (column == iota((GROUP, rows), 1)).astype(BF16)
    picked_hidden = dot(pick, hidden)
    wide_v[:, 2 * LANES :] = jnp.zeros((GROUP, LANES), F32)
    for name in ("wq", "sqk"):
        loads[name].wait()
    gains = sqk_v[...].reshape(1, width)
    wide_v[:, :width] = head_unit(dot_t(picked_hidden.astype(BF16), wqkv_v[0]), gains, same_head)
    xq2[me_far] = pack_heads(wide_v[...])
    pl.semaphore_wait(barrier, near + far + heads - 3)
    arrive = exchange(0, xq2, far, me_far, far_peer)
    query = head_unit(dot_t(hidden, wqkv_v[0]), gains, same_head).astype(BF16)

    loads["wk"].wait()
    key = head_unit(dot_t(hidden, wqkv_v[1]), gains, same_head).astype(BF16)
    loads["wv"].wait()
    value = dot_t(hidden, wqkv_v[2]).astype(BF16)
    picked_key = dot(pick, key).astype(BF16)
    picked_value = dot(pick, value).astype(BF16)
    query_rows = jnp.where(own_lanes, dot(spread, query), 0.0)
    qbd_v[...] = query_rows
    own = scale * jnp.sum(query_rows * dot(spread, key), axis=-1, keepdims=True)
    vb_v[...] = dot(spread, value)
    loads["lens"].wait()
    loads["sk"].wait()
    slots = sk_v.shape[2]
    for r in range(rows):
        block = slice(r * GROUP, (r + 1) * GROUP)
        part = scale * dot(qbd_v[block, :].astype(BF16), sk_v[r])
        s_v[block, :] = jnp.where(iota((GROUP, slots), 1) < lens_s[r], part, LOW)

    arrive()

    def sum_slots(ref, count):
        acc = ref[0].astype(F32)
        for i in range(1, count):
            acc = acc + ref[i].astype(F32)
        return acc

    xq1[me_near] = sum_slots(xq2, far).astype(BF16)
    arrive = exchange(1, xq1, near, me_near, near_peer)

    scores = s_v[...]
    top = jnp.maximum(jnp.max(scores, axis=-1, keepdims=True), own)
    weights = jnp.exp(scores - top)
    own_weight = jnp.exp(own - top)
    share = 1.0 / (jnp.sum(weights, axis=-1, keepdims=True) + own_weight)
    s_v[...] = weights
    loads["sv"].wait()
    for r in range(rows):
        block = slice(r * GROUP, (r + 1) * GROUP)
        o_v[block, :] = dot_t(s_v[block, :].astype(BF16), sv_v[r])
    summed = o_v[...] + own_weight.astype(BF16).astype(F32) * vb_v[...]
    blocks = jnp.where(own_lanes, summed * share, 0.0).astype(BF16)
    attended = dot(gather, blocks).astype(BF16)
    loads["wout"].wait()
    ys1[me_head] = dot(attended, wout_v[...]).astype(BF16)
    short_arrive = exchange(2, ys1, heads, me_head, head_peer)

    loads["lk"].wait()
    loads["lv"].wait()
    arrive()
    queries = sum_slots(xq1, near)

    def unpack_heads(first, second):
        wide_v[:, :LANES] = first
        wide_v[:, LANES : 2 * LANES] = pltpu.roll(first, 4, 0)
        wide_v[:, 2 * LANES :] = second
        return jnp.where(iota((GROUP, width), 0) < 4, wide_v[:, :width], 0.0).astype(BF16)

    long_query = unpack_heads(queries[:GROUP], queries[GROUP:])
    long_rows = jnp.where(lown_lanes, dot(lspread, long_query), 0.0)
    lqbd_v[...] = long_rows
    for i in range(longs):
        block = slice(i * GROUP, (i + 1) * GROUP)
        ls_v[block, :] = scale * dot(lqbd_v[block, :].astype(BF16), lk_v[i])
    place = jnp.full((ltotal, 1), -1, jnp.int32)
    for i in range(longs):
        place = jnp.where(iota((ltotal, 1), 0) // GROUP == i, local[i], place)
    owner = (place >= 0) & (place < rows)
    long_own = scale * jnp.sum(long_rows * dot(lspread, picked_key), axis=-1, keepdims=True)
    long_own = jnp.where(owner, long_own, LOW)
    long_scores = ls_v[...]
    long_top = jnp.maximum(jnp.max(long_scores, axis=-1, keepdims=True), long_own)
    long_weights = jnp.exp(long_scores - long_top)
    long_own_weight = jnp.where(owner, jnp.exp(long_own - long_top), 0.0)
    long_total = jnp.sum(long_weights, axis=-1, keepdims=True) + long_own_weight
    ls_v[...] = long_weights
    for i in range(longs):
        block = slice(i * GROUP, (i + 1) * GROUP)
        lo_v[block, :] = dot_t(ls_v[block, :].astype(BF16), lv_v[i])
    long_summed = lo_v[...] + long_own_weight.astype(BF16).astype(F32) * dot(lspread, picked_value)
    long_blocks = jnp.where(lown_lanes, long_summed / long_total, 0.0).astype(BF16)
    tops = split3(long_top + jnp.log(long_total))
    wide_lane = iota((ltotal, LANES), 1) - HEAD_DIM - iota((ltotal, LANES), 0) % GROUP
    placed = jnp.zeros((ltotal, LANES), F32)
    for i in range(3):
        placed = jnp.where(wide_lane == i * GROUP, tops[i], placed)
    wide_v[:, 2 * LANES :] = dot(lgather, placed.astype(BF16))
    wide_v[:, :width] = dot(lgather, long_blocks)
    xp1[me_near] = pack_heads(wide_v[...])
    arrive = exchange(3, xp1, near, me_near, near_peer)

    for name in ("aat", "wgu", "sgate", "sup", "wdn", "aml"):
        loads[name].wait()
    alpha_attn = aat_v[...].reshape(1, -1)
    alpha_mlp = aml_v[...].reshape(1, -1)
    gate_gain = sgate_v[...].reshape(1, -1)
    up_gain = sup_v[...].reshape(1, -1)

    def update(summed, base, alpha):
        return row_norm(base + alpha * (row_norm(summed) - base)).astype(BF16)

    def feed_forward(middle):
        gate = dot(middle, wgu_v[0]) * gate_gain
        upward = dot(middle, wgu_v[1]) * up_gain
        gated = (gate / (1.0 + jnp.exp(-gate)) * upward).astype(BF16)
        return dot(gated, wdn_v[...])

    short_arrive()
    mid_v[...] = update(sum_slots(ys1, heads), hidden.astype(F32), alpha_attn)

    def merge(ref, count):
        firsts, seconds, sums = [], [], []
        for i in range(count):
            both = ref[i].astype(F32)
            second = both[GROUP:]
            firsts.append(both[:GROUP])
            seconds.append(second)
            sums.append(
                second + pltpu.roll(second, LANES - GROUP, 1) + pltpu.roll(second, LANES - 2 * GROUP, 1)
            )
        most = functools.reduce(jnp.maximum, sums)
        parts = [jnp.exp(s - most) for s in sums]
        whole = functools.reduce(jnp.add, parts)
        out_first = jnp.zeros((GROUP, LANES), F32)
        out_second = jnp.zeros((GROUP, LANES), F32)
        for i in range(count):
            ratio = parts[i] / whole
            turned = pltpu.roll(pltpu.roll(ratio, 4, 0), LANES - 2, 1)
            mixed = jnp.where(sub < 4, ratio, turned)
            left = mixed[:, HEAD_DIM : HEAD_DIM + 1]
            right = mixed[:, HEAD_DIM + 1 : HEAD_DIM + 2]
            out_first = out_first + jnp.where(lane < HEAD_DIM, left, right) * firsts[i]
            out_second = out_second + ratio[:, HEAD_DIM + 4 : HEAD_DIM + 5] * seconds[i]
        return out_first, out_second, most + jnp.log(whole)

    arrive()
    first, second, logs = merge(xp1, near)
    high, middle, low = split3(logs)
    second = jnp.where(lane < HEAD_DIM, second, 0.0)
    lanes_of = ((0, high), (1, pltpu.roll(middle, GROUP, 1)), (2, pltpu.roll(low, 2 * GROUP, 1)))
    for i, term in lanes_of:
        inside = (lane >= HEAD_DIM + i * GROUP) & (lane < HEAD_DIM + (i + 1) * GROUP)
        second = jnp.where(inside, term, second)
    xp2[me_far] = jnp.concatenate([first, second], axis=0).astype(BF16)
    arrive = exchange(4, xp2, far, me_far, far_peer)

    ys2[me_head] = feed_forward(mid_v[...]).astype(BF16)
    short_arrive = exchange(5, ys2, heads, me_head, head_peer)

    half = hidden.shape[1] // 2

    def pack_rows(values):
        upper = iota((GROUP, half), 0) < 4
        return jnp.where(upper, values[:, :half], pltpu.roll(values[:, half:], 4, 0)).astype(BF16)

    def unpack_rows(packed):
        return jnp.concatenate([packed, pltpu.roll(packed, 4, 0)], axis=1)

    arrive()
    first, second, _ = merge(xp2, far)
    long_attended = unpack_heads(first, second)
    yl1[me_head] = pack_rows(dot(long_attended, wout_v[...]))
    arrive = exchange(6, yl1, heads, me_head, head_peer)

    short_arrive()
    new_v[...] = update(sum_slots(ys2, heads), mid_v[...].astype(F32), alpha_mlp)

    arrive()
    long_middle = update(unpack_rows(sum_slots(yl1, heads)), picked_hidden, alpha_attn)
    yl2[me_head] = pack_rows(feed_forward(long_middle))
    arrive = exchange(7, yl2, heads, me_head, head_peer)
    arrive()
    long_new = update(unpack_rows(sum_slots(yl2, heads)), long_middle.astype(F32), alpha_mlp).astype(F32)
    result = new_v[...].astype(F32)
    for i in range(longs):
        here = iota((rows, result.shape[1]), 0) == local[i]
        result = jnp.where(here, long_new[i : i + 1, :], result)
    out_ref[...] = result.astype(BF16)
    for copy in sent:
        copy.wait_send()


def on_device(
    near,
    far,
    heads,
    hidden,
    w_qkv,
    w_out,
    s_qk,
    alpha_attn,
    w_gate_up,
    w_down,
    s_up,
    s_gate,
    alpha_mlp,
    short_keys,
    short_values,
    cache_lengths,
    long_keys,
    long_values,
    long_rows,
):
    def turned(array):
        return jnp.transpose(array, (0, 2, 1))

    arguments = (
        long_rows, cache_lengths, hidden, turned(w_qkv), s_qk, turned(short_keys), turned(short_values),
        turned(long_keys), turned(long_values), w_out, alpha_attn, w_gate_up, s_gate, s_up, w_down, alpha_mlp,
    )
    arguments = tuple(pltpu.with_memory_space_constraint(a, pltpu.HBM) for a in arguments)
    rows, model = hidden.shape
    width = w_qkv.shape[2]
    slots, longs, span = short_keys.shape[1], long_keys.shape[0], long_keys.shape[1]
    copies = [
        (pltpu.SMEM if a.dtype == jnp.int32 else pltpu.VMEM)(a.shape, a.dtype) for a in arguments
    ]
    return pl.pallas_call(
        functools.partial(kernel, near, far, heads),
        out_shape=jax.ShapeDtypeStruct(hidden.shape, BF16),
        in_specs=[pl.BlockSpec(memory_space=pltpu.HBM)] * len(arguments),
        out_specs=pl.BlockSpec(memory_space=pltpu.VMEM),
        scratch_shapes=copies
        + [
            pltpu.VMEM((rows * GROUP, width), F32),
            pltpu.VMEM((rows * GROUP, width), F32),
            pltpu.VMEM((rows * GROUP, slots), F32),
            pltpu.VMEM((rows * GROUP, width), F32),
            pltpu.VMEM((longs * GROUP, width), F32),
            pltpu.VMEM((longs * GROUP, span), F32),
            pltpu.VMEM((longs * GROUP, width), F32),
            pltpu.VMEM((GROUP, 3 * LANES), F32),
            pltpu.VMEM((rows, width), BF16),
            pltpu.VMEM((rows, model), BF16),
            pltpu.VMEM((rows, model), BF16),
            pltpu.VMEM((near, 2 * GROUP, LANES), BF16),
            pltpu.VMEM((far, 2 * GROUP, LANES), BF16),
            pltpu.VMEM((near, 2 * GROUP, LANES), BF16),
            pltpu.VMEM((far, 2 * GROUP, LANES), BF16),
            pltpu.VMEM((heads, rows, model), BF16),
            pltpu.VMEM((heads, rows, model), BF16),
            pltpu.VMEM((heads, GROUP, model // 2), BF16),
            pltpu.VMEM((heads, GROUP, model // 2), BF16),
            pltpu.SemaphoreType.DMA((len(arguments) + 2,)),
            pltpu.SemaphoreType.DMA((8, 8)),
            pltpu.SemaphoreType.DMA((8, 8)),
        ],
        compiler_params=pltpu.CompilerParams(collective_id=0, has_side_effects=True, vmem_limit_bytes=40 * 2**20),
    )(*arguments)


def solution(mesh):
    reqs, heads = mesh.shape["req"], mesh.shape["head"]
    near = math.gcd(NEAR, reqs)
    return jax.shard_map(
        functools.partial(on_device, near, reqs // near, heads),
        mesh=mesh,
        in_specs=(
            P("req", None),
            P(None, None, "head"),
            P("head", None),
            P("head"),
            P(),
            P(None, None, "head"),
            P("head", None),
            P("head"),
            P("head"),
            P(),
            P("req", None, "head"),
            P("req", None, "head"),
            P("req"),
            P(None, "req", "head"),
            P(None, "req", "head"),
            P(),
        ),
        out_specs=P("req", None),
        check_vma=False,
    )
```
